32 devices in a mesh: grp: 2 (over y), seq: 4 (over z), head: 2 (over x), rep: 2 (over core).
Axes of the slice: x: 2, y: 2, z: 4, core: 2. Of those that a mesh axis runs over, the one named last changes fastest.
Arguments:
- query_latent: bfloat16 [1024, 32, 512], P(('grp', 'seq'), ('head', 'rep')), parts along dimension 0, may hold values from -400 to 400
- query_rope: bfloat16 [1024, 2048], P(('grp', 'seq'), ('head', 'rep')), parts along dimension 0, may hold values from -4 to 4
- latent: bfloat16 [8192, 512], P(('grp', 'seq', 'rep')), parts along dimension 0, may hold values from -6 to 6
- key_rope: bfloat16 [64, 8192], P(None, ('grp', 'seq', 'rep')), parts along dimension 1, may hold values from -4 to 4
- value_up: bfloat16 [32, 512, 128], P(('head', 'rep')), may hold values from -2.390625 to 2.390625
- out_proj: bfloat16 [4096, 3584], P(('head', 'rep')), may hold values from -0.09375 to 0.09375
Outputs:
- output: bfloat16 [1024, 3584], P(('grp', 'seq', 'head', 'rep')), parts along dimension 0
The draws below stay inside these ranges and needn't reach their ends.
There are 2 independent parts, one for each index of `grp`. The reference program is written for one: setup_inputs(seed, part) draws one part's arguments, and reference() takes and returns one part's arrays. A program takes and returns all parts, laid end to end along the dimension named above; an argument that names none is the same for every part. Nothing has to cross between parts.
All inputs are finite; a program needn't handle non-finite values.
Results may differ from the reference program's by a relative error of at most 0.017.
Values may be sent and summed in bfloat16 or wider, within the bound.
No kernel may reach another device: no remote copies, remote signals or barrier semaphores. Data moves between devices by JAX's collectives and lax.ppermute only.
A program may use at most 128 MiB of HBM per device.

```python
import jax
import jax.numpy as jnp
from jax import lax

H = 32
D = 3584
DL = 512
DR = 64
VD = 128
Q_DEV = 128
KB = 1024
TOKENS = 4096
QTOK = 512
N_SEQ = 4


def joint_draw(key):
    lat_key = jax.random.fold_in(key, 7001)
    query_key = jax.random.fold_in(key, 7002)
    tokens = KB * N_SEQ
    queries = Q_DEV * N_SEQ
    latents = jnp.clip(jax.random.normal(lat_key, (tokens, DL), jnp.float32), -4.0, 4.0)
    query_values = jnp.clip(jax.random.normal(query_key, (queries, H, DL), jnp.float32), -4.0, 4.0)
    return (latents, query_values)


def draw_query_latent(key, part):
    latents, query_values = joint_draw(key)
    return query_values.astype(jnp.bfloat16)


def draw_latent(key, part):
    latents, query_values = joint_draw(key)
    return latents.astype(jnp.bfloat16)


def steps_of(key, shape, split, smallest, largest):
    level = 1.0
    for dim, shards_of in split:
        heights = jax.random.uniform(jax.random.fold_in(jax.random.fold_in(key, 6), dim), (shards_of,), jnp.float32, smallest / len(split), largest / len(split))
        level = level * jnp.repeat(jnp.exp(heights), shape[dim] // shards_of).reshape((-1,) + (1,) * (len(shape) - 1 - dim))
    return level


def normal_values(stream_key, dims, deviation, limit, cuts=(), kind=jnp.bfloat16):
    array = deviation * jax.random.normal(stream_key, dims, jnp.float32)
    if cuts:
        array = array * steps_of(stream_key, dims, cuts, -0.22, 0.18)
    return jnp.clip(array, -limit, limit).astype(kind)


def setup_inputs(seed: int = 0, part: int = 0) -> dict:
    arg_keys = jax.random.split(jax.random.key(seed), 7)
    part_keys = jax.random.split(jax.random.fold_in(arg_keys[6], part), 7)
    return {
        "query_latent": draw_query_latent(jax.random.fold_in(jax.random.fold_in(arg_keys[6], part), 71), part),
        "query_rope": normal_values(part_keys[1], (QTOK, H * DR), 1.0, 4.0, ((0, 4), (1, 4))),
        "latent": draw_latent(jax.random.fold_in(jax.random.fold_in(arg_keys[6], part), 71), part),
        "key_rope": normal_values(part_keys[3], (DR, TOKENS), 1.0, 4.0, ((1, 8),)),
        "value_up": normal_values(arg_keys[4], (H, DL, VD), 0.4, 2.390625, ((0, 4),)),
        "out_proj": normal_values(arg_keys[5], (H * VD, D), (H * VD) ** -0.5, 0.09375, ((0, 4),)),
    }


def reference(query_latent, query_rope, latent, key_rope, value_up, out_proj):
    levels = min(4, N_SEQ // 4 + 1)
    score_scale = (DL + DR) ** -0.5
    query_index = jnp.arange(Q_DEV, dtype=jnp.int32)
    key_index = jnp.arange(KB, dtype=jnp.int32)

    def one_shard(shard_index):
        queries = lax.dynamic_slice_in_dim(query_latent, (shard_index * Q_DEV).astype(jnp.int32), Q_DEV, 0).astype(jnp.float32)
        rope_queries = lax.dynamic_slice_in_dim(query_rope, (shard_index * Q_DEV).astype(jnp.int32), Q_DEV, 0)
        rope_queries = rope_queries.reshape(Q_DEV, H, DR).astype(jnp.float32)
        latents = [lax.dynamic_slice_in_dim(latent, (shard_index * KB).astype(jnp.int32), KB, 0)]
        rope_blocks = [lax.dynamic_slice_in_dim(key_rope, (shard_index * KB).astype(jnp.int32), KB, 1)]
        allowed = [key_index[None, :] <= (KB - Q_DEV + query_index)[:, None]]
        for level_index in range(levels):
            source = shard_index - 2 ** level_index
            block_start = (jnp.maximum(source, 0) * KB).astype(jnp.int32)
            latents.append(lax.dynamic_slice_in_dim(latent, block_start, KB, 0))
            rope_blocks.append(lax.dynamic_slice_in_dim(key_rope, block_start, KB, 1))
            allowed.append(jnp.broadcast_to(source >= 0, (Q_DEV, KB)))
        key_latent = jnp.concatenate(latents, axis=0).astype(jnp.float32)
        key_ropes = jnp.concatenate(rope_blocks, axis=1).astype(jnp.float32)
        visible = jnp.concatenate(allowed, axis=1)
        scores = jnp.einsum("qhc,kc->hqk", queries, key_latent, precision=lax.Precision.HIGHEST)
        scores = scores + jnp.einsum("qhr,rk->hqk", rope_queries, key_ropes, precision=lax.Precision.HIGHEST)
        scores = jnp.where(visible[None], scores * score_scale, -1.0e30)
        row_max = jnp.max(scores, axis=2, keepdims=True)
        weights = jnp.exp(scores - row_max)
        row_total = jnp.sum(weights, axis=2, keepdims=True)
        rounded = lax.optimization_barrier(weights.astype(jnp.bfloat16)).astype(jnp.float32)
        attended = jnp.einsum("hqk,kc->hqc", rounded, key_latent, precision=lax.Precision.HIGHEST) / row_total
        attended = attended.astype(jnp.bfloat16).astype(jnp.float32)
        expanded = jnp.einsum("hqc,hcv->qhv", attended, value_up.astype(jnp.float32), precision=lax.Precision.HIGHEST)
        expanded = expanded.astype(jnp.bfloat16).reshape(Q_DEV, H * VD)
        return jnp.dot(expanded, out_proj, preferred_element_type=jnp.float32).astype(jnp.bfloat16)

    output = lax.map(one_shard, jnp.arange(N_SEQ, dtype=jnp.int32))
    return output.reshape(N_SEQ * Q_DEV, D)
```

```python
import functools
import math

import jax
import jax.numpy as jnp
from jax import lax
from jax.experimental import pallas as pl
from jax.experimental.pallas import tpu as pltpu
from jax.sharding import PartitionSpec as P

masked_score = -1e30
lanes = 128
log2e = math.log2(math.e)
in_vmem = pl.BlockSpec(memory_space=pltpu.VMEM)
in_smem = pl.BlockSpec(memory_space=pltpu.SMEM)
anywhere = pl.BlockSpec(memory_space=pl.ANY)
contract_last = (((1,), (1,)), ((), ()))


def params(mib):
    return pltpu.CompilerParams(vmem_limit_bytes=mib << 20)


def shifted(value, axis, by):
    peers = lax.axis_size(axis)
    return lax.ppermute(value, axis, [(i, i + by) for i in range(peers) if 0 <= i + by < peers])


def rotated(value, axis, by):
    peers = lax.axis_size(axis)
    return lax.ppermute(value, axis, [(i, (i + by) % peers) for i in range(peers)])


def pack_kernel(part_ref, latent_ref, rope_ref, packed_ref, sems):
    width = latent_ref.shape[1]
    rope_width = rope_ref.shape[0]
    rows = packed_ref.shape[0] * width // (width + rope_width)
    folds = width // rows
    group = rope_width // folds
    start = pl.multiple_of(part_ref[0] * rows, rows)
    copies = [
        pltpu.make_async_copy(
            latent_ref.at[pl.ds(start, rows), :], packed_ref.at[pl.ds(0, rows), :], sems.at[0]
        )
    ]
    for fold in range(folds):
        copies.append(
            pltpu.make_async_copy(
                rope_ref.at[pl.ds(fold * group, group), pl.ds(start, rows)],
                packed_ref.at[pl.ds(rows, group), pl.ds(fold * rows, rows)],
                sems.at[fold + 1],
            )
        )
    for copy in copies:
        copy.start()
    for copy in copies:
        copy.wait()


def pack_part(part, parts, latent, key_rope):
    rows = latent.shape[0] // parts
    width = latent.shape[1]
    folds = width // rows
    group = key_rope.shape[0] // folds
    return pl.pallas_call(
        pack_kernel,
        out_shape=jax.ShapeDtypeStruct((rows + group, width), latent.dtype),
        in_specs=[in_smem, anywhere, anywhere],
        out_specs=in_vmem,
        scratch_shapes=[pltpu.SemaphoreType.DMA((folds + 1,))],
        compiler_params=params(4),
        cost_estimate=pl.CostEstimate(flops=0, bytes_accessed=600000, transcendentals=0),
        name="pack_part",
    )(part, latent, key_rope)


def read_piece(ref, rope_width):
    width = ref.shape[1]
    rows = ref.shape[0] * width // (width + rope_width)
    folds = width // rows
    group = rope_width // folds
    keys = ref[pl.ds(0, rows), :]
    ropes = [ref[pl.ds(rows, group), pl.ds(fold * rows, rows)] for fold in range(folds)]
    return keys, jnp.concatenate(ropes, axis=0)


def attend_rows(rows_here, query_ref, rope_ref, pieces, scale, state):
    query = query_ref[rows_here, :]
    rope = rope_ref[rows_here, :]
    scores = []
    for keys, ropes, mask, bias in pieces:
        score = lax.dot_general(query, keys, contract_last, preferred_element_type=jnp.float32)
        score = score + jnp.dot(rope, ropes, preferred_element_type=jnp.float32)
        if mask is not None:
            score = mask(score)
        scores.append(score)
    tops = []
    for score, (_, _, _, bias) in zip(scores, pieces):
        top = jnp.max(score, axis=1, keepdims=True) * scale
        tops.append(top if bias is None else top + bias)
    new_max = functools.reduce(jnp.maximum, tops)
    if state is not None:
        new_max = jnp.maximum(new_max, state[0])
    total = None
    out = None
    for score, (keys, _, _, bias) in zip(scores, pieces):
        shift = new_max if bias is None else new_max - bias
        weights = jnp.exp2(score * scale - shift)
        part = jnp.sum(weights, axis=1, keepdims=True)
        update = jnp.dot(weights.astype(keys.dtype), keys, preferred_element_type=jnp.float32)
        total = part if total is None else total + part
        out = update if out is None else out + update
    if state is not None:
        factor = jnp.exp2(state[0] - new_max)
        total = total + state[1] * factor
        out = out + state[2] * factor
    return new_max, total, out


def own_kernel(block, heads, scale, rep_ref, query_ref, qrope_ref, *refs):
    here_latent, here_rope, there_latent, there_rope, max_ref, sum_ref, out_ref = refs
    rows = query_ref.shape[0]
    half = here_latent.shape[0]
    queries = rows // heads

    for start in range(0, rows, block):
        rows_here = pl.ds(start, block)

        def causal(first, score):
            block_rows = 2 * half
            j = first + lax.broadcasted_iota(jnp.int32, score.shape, 1)
            q = (start + lax.broadcasted_iota(jnp.int32, score.shape, 0)) // heads
            return jnp.where(j <= block_rows - queries + q, score, masked_score)

        rep = rep_ref[0]
        pieces = [
            (here_latent[...], here_rope[...], functools.partial(causal, rep * half), None),
            (there_latent[...], there_rope[...], functools.partial(causal, (1 - rep) * half), None),
        ]
        state = attend_rows(rows_here, query_ref, qrope_ref, pieces, scale, None)
        max_ref[rows_here, :], sum_ref[rows_here, :], out_ref[rows_here, :] = state


def attention_cost(rows, keys, width):
    return pl.CostEstimate(
        flops=4 * rows * keys * width, bytes_accessed=2 * rows * width, transcendentals=rows * keys
    )


def attend_own(rep, query, query_rope, here, there, heads, scale):
    rows, width = query.shape
    out_shape = (
        jax.ShapeDtypeStruct((rows, 1), jnp.float32),
        jax.ShapeDtypeStruct((rows, 1), jnp.float32),
        jax.ShapeDtypeStruct((rows, width), jnp.float32),
    )
    return pl.pallas_call(
        functools.partial(own_kernel, math.gcd(rows, 256), heads, scale),
        out_shape=out_shape,
        in_specs=[in_smem] + [in_vmem] * 6,
        out_specs=[in_vmem] * 3,
        compiler_params=params(32),
        cost_estimate=attention_cost(rows, 2 * here[0].shape[0], width),
        name="attend_own",
    )(rep, query, query_rope, *here, *there)


def biased_pieces(levels_of, bias_ref, refs, rope_width):
    pieces = []
    for level, ref in zip(levels_of, refs):
        keys, ropes = read_piece(ref, rope_width)
        pieces.append((keys, ropes, None, bias_ref[level]))
    return pieces


def middle_kernel(block, levels_of, scale, bias_ref, query_ref, qrope_ref, *refs):
    count = len(levels_of)
    max_in, sum_in, out_in, max_ref, sum_ref, out_ref = refs[count:]
    rope_width = qrope_ref.shape[1]
    for start in range(0, query_ref.shape[0], block):
        rows_here = pl.ds(start, block)
        pieces = biased_pieces(levels_of, bias_ref, refs[:count], rope_width)
        state = (max_in[rows_here, :], sum_in[rows_here, :], out_in[rows_here, :])
        state = attend_rows(rows_here, query_ref, qrope_ref, pieces, scale, state)
        max_ref[rows_here, :], sum_ref[rows_here, :], out_ref[rows_here, :] = state


def attend_middle(bias, query, query_rope, pieces, levels_of, state, scale):
    rows, width = query.shape
    keys = sum(piece.shape[0] for piece in pieces)
    return pl.pallas_call(
        functools.partial(middle_kernel, math.gcd(rows, 256), tuple(levels_of), scale),
        out_shape=tuple(jax.ShapeDtypeStruct(s.shape, s.dtype) for s in state),
        in_specs=[in_smem] + [in_vmem] * (2 + len(pieces) + 3),
        out_specs=[in_vmem] * 3,
        compiler_params=params(32),
        cost_estimate=attention_cost(rows, keys, width),
        name="attend_middle",
    )(bias, query, query_rope, *pieces, *state)


def last_kernel(block, levels_of, heads, scale, peers, order_ref, bias_ref, query_ref, qrope_ref, *refs):
    count = len(levels_of)
    max_in, sum_in, out_in, up_ref, proj_ref, result_ref, norm_ref, exp_ref = refs[count:]
    rope_width = qrope_ref.shape[1]
    rows, width = query_ref.shape
    queries = rows // heads
    value = up_ref.shape[2]
    for start in range(0, rows, block):
        rows_here = pl.ds(start, block)
        pieces = biased_pieces(levels_of, bias_ref, refs[:count], rope_width)
        state = (max_in[rows_here, :], sum_in[rows_here, :], out_in[rows_here, :])
        _, total, out = attend_rows(rows_here, query_ref, qrope_ref, pieces, scale, state)
        norm = out * (1.0 / total)
        for tile in range(width // lanes):
            norm_ref[tile, rows_here, :] = norm[:, tile * lanes : (tile + 1) * lanes]
    for head in range(heads):
        tiles = [
            norm_ref[tile, pl.ds(head, queries, stride=heads), :].astype(jnp.bfloat16)
            for tile in range(width // lanes)
        ]
        attended = jnp.concatenate(tiles, axis=1)
        expanded = jnp.dot(attended, up_ref[head], preferred_element_type=jnp.float32)
        exp_ref[:, pl.ds(head * value, value)] = expanded.astype(jnp.bfloat16)
    chunk = queries // peers
    parts = [exp_ref[pl.ds(pl.multiple_of(order_ref[i] * chunk, chunk), chunk), :] for i in range(peers)]
    lhs = jnp.concatenate(parts, axis=0)
    columns = proj_ref.shape[1]
    step = math.gcd(columns, 512)
    for column in range(0, columns, step):
        piece = jnp.dot(lhs, proj_ref[:, pl.ds(column, step)], preferred_element_type=jnp.float32)
        result_ref[:, pl.ds(column, step)] = piece.astype(result_ref.dtype)


def attend_last(order, bias, query, query_rope, pieces, levels_of, state, scale, value_up, out_proj):
    rows, width = query.shape
    heads = value_up.shape[0]
    queries = rows // heads
    keys = sum(piece.shape[0] for piece in pieces)
    columns = out_proj.shape[1]
    return pl.pallas_call(
        functools.partial(
            last_kernel, math.gcd(rows, 256), tuple(levels_of), heads, scale, order.shape[0]
        ),
        out_shape=jax.ShapeDtypeStruct((queries, columns), jnp.bfloat16),
        in_specs=[in_smem, in_smem] + [in_vmem] * (2 + len(pieces) + 3 + 2),
        out_specs=in_vmem,
        scratch_shapes=[
            pltpu.VMEM((width // lanes, rows, lanes), jnp.float32),
            pltpu.VMEM((queries, out_proj.shape[0]), jnp.bfloat16),
        ],
        compiler_params=params(40),
        cost_estimate=attention_cost(rows, keys, width),
        name="attend_last",
    )(order, bias, query, query_rope, *pieces, *state, value_up, out_proj)


def shards(query_latent, query_rope, latent, key_rope, value_up, out_proj):
    queries, heads, width = query_latent.shape
    rope_width = key_rope.shape[0]
    levels = min(4, lax.axis_size("seq") // 4 + 1)
    columns = lax.axis_size("head")
    column = lax.axis_index("head")
    rep = lax.axis_index("rep")
    shard_index = lax.axis_index("seq")
    scale = (width + rope_width) ** (-0.5) * log2e
    bias = jnp.stack(
        [jnp.where(shard_index >= 2**level, 0.0, masked_score) for level in range(levels)]
    ).astype(jnp.float32)
    query = query_latent.reshape(queries * heads, width)
    qrope = query_rope.reshape(queries * heads, rope_width)

    part = pack_part(column[None], columns, latent, key_rope)
    by_level = []
    moved = part
    for level in range(levels):
        moved = shifted(moved, "seq", 1 if level == 0 else 2 ** (level - 1))
        by_level.append(moved)
    there = (rotated(latent, "rep", 1), rotated(key_rope, "rep", 1))
    state = attend_own(rep[None], query, qrope, (latent, key_rope), there, heads, scale)

    middle, middle_levels, last, last_levels = [], [], [], []
    for level in range(levels):
        direct = by_level[level]
        crossed = [rotated(direct, "head", by) for by in range(1, columns)]
        for index, piece in enumerate([direct] + crossed):
            both = [piece, rotated(piece, "rep", 1)]
            if level == levels - 1 and index > 0:
                last += both
                last_levels += [level] * 2
            else:
                middle += both
                middle_levels += [level] * 2
    state = attend_middle(bias, query, qrope, middle, middle_levels, state, scale)

    chips = [(column + by) % columns for by in range(1, columns + 1)]
    order = jnp.stack([chip * 2 + 1 - rep for chip in chips] + [chip * 2 + rep for chip in chips])
    partial = attend_last(
        order, bias, query, qrope, last, last_levels, state, scale, value_up, out_proj
    )
    half = queries // 2
    arrived = rotated(partial[:half], "rep", 1)
    chunk = half // columns
    kept = partial[half:]
    sums = []
    for index in range(columns):
        rows = slice(index * chunk, (index + 1) * chunk)
        sums.append(kept[rows].astype(jnp.float32) + arrived[rows].astype(jnp.float32))
    result = sums[-1]
    for index in range(columns - 1):
        result = result + rotated(sums[index].astype(jnp.bfloat16), "head", index + 1).astype(
            jnp.float32
        )
    return result.astype(jnp.bfloat16)


def solution(mesh):
    placed = (
        P(("grp", "seq"), ("head", "rep"), None),
        P(("grp", "seq"), ("head", "rep")),
        P(("grp", "seq", "rep"), None),
        P(None, ("grp", "seq", "rep")),
        P(("head", "rep"), None, None),
        P(("head", "rep"), None),
    )
    return jax.shard_map(
        shards,
        mesh=mesh,
        in_specs=placed,
        out_specs=P(("grp", "seq", "head", "rep"), None),
        check_vma=False,
    )
```

```python
import functools
import math

import jax
import jax.numpy as jnp
from jax import lax
from jax.experimental import pallas as pl
from jax.experimental.pallas import tpu as pltpu
from jax.sharding import PartitionSpec as P


masked_score = -1e30
lanes = 128
log2e = math.log2(math.e)
in_vmem = pl.BlockSpec(memory_space=pltpu.VMEM)
in_smem = pl.BlockSpec(memory_space=pltpu.SMEM)
in_hbm = pl.BlockSpec(memory_space=pltpu.HBM)
contract_last = (((1,), (1,)), ((), ()))


def kept_in_hbm(value):
    return pltpu.with_memory_space_constraint(value, pltpu.HBM)


def params(mib):
    return pltpu.CompilerParams(vmem_limit_bytes=mib << 20)


def shifted(value, axis, by, first):
    peers = lax.axis_size(axis)
    return lax.ppermute(value, axis, [(i, i + by) for i in range(first, peers - by)])


def rotated(value, axis, by):
    peers = lax.axis_size(axis)
    return lax.ppermute(value, axis, [(i, (i + by) % peers) for i in range(peers)])


def pack_kernel(part_ref, latent_ref, rope_ref, packed_ref, sems):
    width = latent_ref.shape[1]
    rope_width = rope_ref.shape[0]
    rows = packed_ref.shape[0] * width // (width + rope_width)
    folds = width // rows
    group = rope_width // folds
    start = pl.multiple_of(part_ref[0] * rows, rows)
    copies = [
        pltpu.make_async_copy(
            latent_ref.at[pl.ds(start, rows), :], packed_ref.at[pl.ds(0, rows), :], sems.at[0]
        )
    ]
    for fold in range(folds):
        copies.append(
            pltpu.make_async_copy(
                rope_ref.at[pl.ds(fold * group, group), pl.ds(start, rows)],
                packed_ref.at[pl.ds(rows, group), pl.ds(fold * rows, rows)],
                sems.at[fold + 1],
            )
        )
    for copy in copies:
        copy.start()
    for copy in copies:
        copy.wait()


def pack_part(part, parts, latent, key_rope):
    rows = latent.shape[0] // parts
    width = latent.shape[1]
    folds = width // rows
    group = key_rope.shape[0] // folds
    return pl.pallas_call(
        pack_kernel,
        out_shape=jax.ShapeDtypeStruct((rows + group, width), latent.dtype),
        in_specs=[in_smem, in_hbm, in_hbm],
        out_specs=in_vmem,
        scratch_shapes=[pltpu.SemaphoreType.DMA((folds + 1,))],
        compiler_params=params(4),
        cost_estimate=pl.CostEstimate(flops=0, bytes_accessed=600000, transcendentals=0),
        name="pack_part",
    )(part, kept_in_hbm(latent), kept_in_hbm(key_rope))


def read_piece(ref, rope_width):
    width = ref.shape[1]
    rows = ref.shape[0] * width // (width + rope_width)
    folds = width // rows
    group = rope_width // folds
    keys = ref[pl.ds(0, rows), :]
    ropes = [ref[pl.ds(rows, group), pl.ds(fold * rows, rows)] for fold in range(folds)]
    return keys, jnp.concatenate(ropes, axis=0)


def attend_rows(rows_here, query_ref, rope_ref, pieces, scale, state):
    query = query_ref[rows_here, :]
    rope = rope_ref[rows_here, :]
    scores = []
    for keys, ropes, mask, bias in pieces:
        score = lax.dot_general(query, keys, contract_last, preferred_element_type=jnp.float32)
        score = score + jnp.dot(rope, ropes, preferred_element_type=jnp.float32)
        if mask is not None:
            score = mask(score)
        scores.append(score)
    tops = []
    for score, (_, _, _, bias) in zip(scores, pieces):
        top = jnp.max(score, axis=1, keepdims=True) * scale
        tops.append(top if bias is None else top + bias)
    new_max = functools.reduce(jnp.maximum, tops)
    if state is not None:
        new_max = jnp.maximum(new_max, state[0])
    total = None
    out = None
    for score, (keys, _, _, bias) in zip(scores, pieces):
        shift = new_max if bias is None else new_max - bias
        weights = jnp.exp2(score * scale - shift)
        part = jnp.sum(weights, axis=1, keepdims=True)
        update = jnp.dot(weights.astype(keys.dtype), keys, preferred_element_type=jnp.float32)
        total = part if total is None else total + part
        out = update if out is None else out + update
    if state is not None:
        factor = jnp.exp2(state[0] - new_max)
        total = total + state[1] * factor
        out = out + state[2] * factor
    return new_max, total, out


def own_kernel(block, heads, scale, rep_ref, query_hbm, qrope_ref, latent_hbm, rope_hbm, *refs):
    there_latent, there_rope, query_ref, max_ref, sum_ref, out_ref, latent_ref, rope_ref, sems = refs
    copies = [
        pltpu.make_async_copy(query_hbm, query_ref, sems.at[0]),
        pltpu.make_async_copy(latent_hbm, latent_ref, sems.at[1]),
        pltpu.make_async_copy(rope_hbm, rope_ref, sems.at[2]),
    ]
    for copy in copies:
        copy.start()
    for copy in copies:
        copy.wait()
    rows = query_ref.shape[0]
    half = latent_ref.shape[0]
    queries = rows // heads
    rep = rep_ref[0]

    for start in range(0, rows, block):
        rows_here = pl.ds(start, block)

        def causal(first, score):
            j = first + lax.broadcasted_iota(jnp.int32, score.shape, 1)
            q = (start + lax.broadcasted_iota(jnp.int32, score.shape, 0)) // heads
            return jnp.where(j <= 2 * half - queries + q, score, masked_score)

        pieces = [
            (latent_ref[...], rope_ref[...], functools.partial(causal, rep * half), None),
            (there_latent[...], there_rope[...], functools.partial(causal, (1 - rep) * half), None),
        ]
        state = attend_rows(rows_here, query_ref, qrope_ref, pieces, scale, None)
        max_ref[rows_here, :], sum_ref[rows_here, :], out_ref[rows_here, :] = state


def attention_cost(rows, keys, width):
    return pl.CostEstimate(
        flops=4 * rows * keys * width, bytes_accessed=2 * rows * width, transcendentals=rows * keys
    )


def attend_own(rep, query, query_rope, here, there, heads, scale):
    rows, width = query.shape
    out_shape = (
        jax.ShapeDtypeStruct(query.shape, query.dtype),
        jax.ShapeDtypeStruct((rows, 1), jnp.float32),
        jax.ShapeDtypeStruct((rows, 1), jnp.float32),
        jax.ShapeDtypeStruct((rows, width), jnp.float32),
    )
    query, *state = pl.pallas_call(
        functools.partial(own_kernel, math.gcd(rows, 256), heads, scale),
        out_shape=out_shape,
        in_specs=[in_smem, in_hbm, in_vmem, in_hbm, in_hbm, in_vmem, in_vmem],
        out_specs=[in_vmem] * 4,
        scratch_shapes=[
            pltpu.VMEM(here[0].shape, here[0].dtype),
            pltpu.VMEM(here[1].shape, here[1].dtype),
            pltpu.SemaphoreType.DMA((3,)),
        ],
        compiler_params=params(10),
        cost_estimate=attention_cost(rows, 2 * here[0].shape[0], width),
        name="attend_own",
    )(rep, kept_in_hbm(query), query_rope, *[kept_in_hbm(x) for x in here], *there)
    return query, state


def biased_pieces(levels_of, shard_ref, refs, rope_width):
    pieces = []
    for level, ref in zip(levels_of, refs):
        keys, ropes = read_piece(ref, rope_width)
        bias = jnp.where(shard_ref[0] >= 2**level, 0.0, masked_score)
        pieces.append((keys, ropes, None, bias))
    return pieces


def middle_kernel(block, levels_of, scale, shard_ref, query_ref, qrope_ref, *refs):
    count = len(levels_of)
    max_in, sum_in, out_in, max_ref, sum_ref, out_ref = refs[count:]
    rope_width = qrope_ref.shape[1]
    for start in range(0, query_ref.shape[0], block):
        rows_here = pl.ds(start, block)
        pieces = biased_pieces(levels_of, shard_ref, refs[:count], rope_width)
        state = (max_in[rows_here, :], sum_in[rows_here, :], out_in[rows_here, :])
        state = attend_rows(rows_here, query_ref, qrope_ref, pieces, scale, state)
        max_ref[rows_here, :], sum_ref[rows_here, :], out_ref[rows_here, :] = state


def attend_middle(shard, query, query_rope, pieces, levels_of, state, scale):
    rows, width = query.shape
    keys = sum(piece.shape[0] for piece in pieces)
    return pl.pallas_call(
        functools.partial(middle_kernel, math.gcd(rows, 256), tuple(levels_of), scale),
        out_shape=tuple(jax.ShapeDtypeStruct(s.shape, s.dtype) for s in state),
        in_specs=[in_smem] + [in_vmem] * (2 + len(pieces) + 3),
        out_specs=[in_vmem] * 3,
        compiler_params=params(10),
        cost_estimate=attention_cost(rows, keys, width),
        name="attend_middle",
    )(shard, query, query_rope, *pieces, *state)


def last_kernel(
    block, levels_of, heads, scale, columns, column_ref, rep_ref, shard_ref, query_ref, qrope_ref, *refs
):
    count = len(levels_of)
    max_in, sum_in, out_in, up_ref, proj_ref, result_ref, norm_ref, exp_ref = refs[count:]
    rope_width = qrope_ref.shape[1]
    rows, width = query_ref.shape
    queries = rows // heads
    value = up_ref.shape[2]
    for start in range(0, rows, block):
        rows_here = pl.ds(start, block)
        pieces = biased_pieces(levels_of, shard_ref, refs[:count], rope_width)
        state = (max_in[rows_here, :], sum_in[rows_here, :], out_in[rows_here, :])
        _, total, out = attend_rows(rows_here, query_ref, qrope_ref, pieces, scale, state)
        norm = out * (1.0 / total)
        for tile in range(width // lanes):
            norm_ref[tile, rows_here, :] = norm[:, tile * lanes : (tile + 1) * lanes]
    for head in range(heads):
        tiles = [
            norm_ref[tile, pl.ds(head, queries, stride=heads), :].astype(jnp.bfloat16)
            for tile in range(width // lanes)
        ]
        attended = jnp.concatenate(tiles, axis=1)
        expanded = jnp.dot(attended, up_ref[head], preferred_element_type=jnp.float32)
        exp_ref[:, pl.ds(head * value, value)] = expanded.astype(jnp.bfloat16)
    chunk = queries // (2 * columns)
    parts = []
    for core in (1 - rep_ref[0], rep_ref[0]):
        for by in range(1, columns + 1):
            owner = lax.rem(column_ref[0] + by, columns) * 2 + core
            parts.append(exp_ref[pl.ds(pl.multiple_of(owner * chunk, chunk), chunk), :])
    lhs = jnp.concatenate(parts, axis=0)
    width_out = proj_ref.shape[1]
    step = math.gcd(width_out, 512)
    for start in range(0, width_out, step):
        piece = jnp.dot(lhs, proj_ref[:, pl.ds(start, step)], preferred_element_type=jnp.float32)
        result_ref[:, pl.ds(start, step)] = piece.astype(result_ref.dtype)


def attend_last(columns, column, rep, shard, query, query_rope, pieces, levels_of, state, scale, value_up, out_proj):
    rows, width = query.shape
    heads = value_up.shape[0]
    queries = rows // heads
    keys = sum(piece.shape[0] for piece in pieces)
    width_out = out_proj.shape[1]
    return pl.pallas_call(
        functools.partial(
            last_kernel, math.gcd(rows, 256), tuple(levels_of), heads, scale, columns
        ),
        out_shape=jax.ShapeDtypeStruct((queries, width_out), jnp.bfloat16),
        in_specs=[in_smem] * 3 + [in_vmem] * (2 + len(pieces) + 3 + 2),
        out_specs=in_vmem,
        scratch_shapes=[
            pltpu.VMEM((width // lanes, rows, lanes), jnp.float32),
            pltpu.VMEM((queries, out_proj.shape[0]), jnp.bfloat16),
        ],
        compiler_params=params(12),
        cost_estimate=attention_cost(rows, keys, width),
        name="attend_last",
    )(column, rep, shard, query, query_rope, *pieces, *state, value_up, out_proj)


def shards(query_latent, query_rope, latent, key_rope, value_up, out_proj):
    queries, heads, width = query_latent.shape
    rope_width = key_rope.shape[0]
    levels = level_count(lax.axis_size("seq"))
    columns = lax.axis_size("head")
    column = lax.axis_index("head")[None]
    rep = lax.axis_index("rep")[None]
    shard = lax.axis_index("seq")[None]
    column, rep, shard = lax.optimization_barrier((column, rep, shard))
    scale = (width + rope_width) ** (-0.5) * log2e
    query = query_latent.reshape(queries * heads, width)
    qrope = query_rope.reshape(queries * heads, rope_width)

    part = pack_part(column, columns, latent, key_rope)
    by_level = []
    moved = part
    for level in range(levels):
        by = 1 if level == 0 else 2 ** (level - 1)
        moved = shifted(moved, "seq", by, 0 if level == 0 else by)
        by_level.append(moved)
    there = (rotated(latent, "rep", 1), rotated(key_rope, "rep", 1))
    query, state = attend_own(rep, query, qrope, (latent, key_rope), there, heads, scale)

    middle, middle_levels, last, last_levels = [], [], [], []
    for level in range(levels):
        direct = by_level[level]
        pieces = [direct]
        for by in range(1, columns):
            pieces.append(rotated(direct, "head", by))
        for index, piece in enumerate(pieces):
            both = [piece, rotated(piece, "rep", 1)]
            if level == levels - 1 and index > 0:
                last += both
                last_levels += [level] * 2
            else:
                middle += both
                middle_levels += [level] * 2
    state = attend_middle(shard, query, qrope, middle, middle_levels, state, scale)

    partial = attend_last(
        columns, column, rep, shard, query, qrope, last, last_levels, state, scale, value_up, out_proj
    )
    half = queries // 2
    arrived = rotated(partial[:half], "rep", 1)
    chunk = half // columns
    kept = partial[half:]
    sums = []
    for index in range(columns):
        rows = slice(index * chunk, (index + 1) * chunk)
        sums.append(kept[rows].astype(jnp.float32) + arrived[rows].astype(jnp.float32))
    result = sums[-1]
    for index in range(columns - 1):
        sent = sums[index].astype(jnp.bfloat16)
        result = result + rotated(sent, "head", index + 1).astype(jnp.float32)
    return result.astype(jnp.bfloat16)


def level_count(shards_along):
    return min(4, shards_along // 4 + 1)


def solution(mesh):
    placed = (
        P(("grp", "seq"), ("head", "rep"), None),
        P(("grp", "seq"), ("head", "rep")),
        P(("grp", "seq", "rep"), None),
        P(None, ("grp", "seq", "rep")),
        P(("head", "rep"), None, None),
        P(("head", "rep"), None),
    )

    return jax.shard_map(
        shards,
        mesh=mesh,
        in_specs=placed,
        out_specs=P(("grp", "seq", "head", "rep"), None),
        check_vma=False,
    )
```

```python
import functools
import math

import jax
import jax.numpy as jnp
from jax import lax
from jax.experimental import pallas as pl
from jax.experimental.pallas import tpu as pltpu
from jax.sharding import PartitionSpec as P


masked_score = -1e30
lanes = 128
log2e = math.log2(math.e)
in_vmem = pl.BlockSpec(memory_space=pltpu.VMEM)
in_smem = pl.BlockSpec(memory_space=pltpu.SMEM)
in_hbm = pl.BlockSpec(memory_space=pltpu.HBM)
contract_last = (((1,), (1,)), ((), ()))


def kept_in_hbm(value):
    return pltpu.with_memory_space_constraint(value, pltpu.HBM)


def params(mib):
    return pltpu.CompilerParams(vmem_limit_bytes=mib << 20)


def shifted(value, axis, by, first):
    peers = lax.axis_size(axis)
    return lax.ppermute(value, axis, [(i, i + by) for i in range(first, peers - by)])


def rotated(value, axis, by):
    peers = lax.axis_size(axis)
    return lax.ppermute(value, axis, [(i, (i + by) % peers) for i in range(peers)])


def split_rows(packed_rows, width, rope_width):
    rows = packed_rows * width // (width + rope_width)
    folds = width // rows
    return rows, folds, rope_width // folds


def pack_kernel(part_ref, latent_ref, rope_ref, *refs):
    packed_refs, sems = refs[:-1], refs[-1]
    width = latent_ref.shape[1]
    rows, folds, group = split_rows(packed_refs[0].shape[0], width, rope_ref.shape[0])
    copies = []
    for chunk, packed_ref in enumerate(packed_refs):
        start = pl.multiple_of((part_ref[0] * len(packed_refs) + chunk) * rows, rows)
        moves = [(latent_ref.at[pl.ds(start, rows), :], packed_ref.at[pl.ds(0, rows), :])]
        for fold in range(folds):
            moves.append(
                (
                    rope_ref.at[pl.ds(fold * group, group), pl.ds(start, rows)],
                    packed_ref.at[pl.ds(rows, group), pl.ds(fold * rows, rows)],
                )
            )
        for move in moves:
            copies.append(pltpu.make_async_copy(*move, sems.at[len(copies)]))
    for copy in copies:
        copy.start()
    for copy in copies:
        copy.wait()


def pack_part(part, parts, chunks, latent, key_rope):
    width = latent.shape[1]
    rows = latent.shape[0] // parts // chunks
    folds = width // rows
    packed = jax.ShapeDtypeStruct((rows + key_rope.shape[0] // folds, width), latent.dtype)
    return pl.pallas_call(
        pack_kernel,
        out_shape=[packed] * chunks,
        in_specs=[in_smem, in_hbm, in_hbm],
        out_specs=[in_vmem] * chunks,
        scratch_shapes=[pltpu.SemaphoreType.DMA((chunks * (folds + 1),))],
        compiler_params=params(4),
        cost_estimate=pl.CostEstimate(flops=0, bytes_accessed=600000, transcendentals=0),
        name="pack_part",
    )(part, kept_in_hbm(latent), kept_in_hbm(key_rope))


def joined(refs, rope_width):
    keys, ropes = [], []
    for ref in refs:
        rows, folds, group = split_rows(ref.shape[0], ref.shape[1], rope_width)
        keys.append(ref[pl.ds(0, rows), :])
        parts = [ref[pl.ds(rows, group), pl.ds(fold * rows, rows)] for fold in range(folds)]
        ropes.append(jnp.concatenate(parts, axis=0))
    return jnp.concatenate(keys, axis=0), jnp.concatenate(ropes, axis=1)


def attend_rows(rows_here, query_ref, rope_ref, pieces, scale, state):
    query = query_ref[rows_here, :]
    rope = rope_ref[rows_here, :]
    scores = []
    for keys, ropes, mask, bias in pieces:
        score = lax.dot_general(query, keys, contract_last, preferred_element_type=jnp.float32)
        score = score + jnp.dot(rope, ropes, preferred_element_type=jnp.float32)
        if mask is not None:
            score = mask(score)
        scores.append(score)
    tops = []
    for score, (_, _, _, bias) in zip(scores, pieces):
        top = jnp.max(score, axis=1, keepdims=True) * scale
        tops.append(top if bias is None else top + bias)
    new_max = functools.reduce(jnp.maximum, tops)
    if state is not None:
        new_max = jnp.maximum(new_max, state[0])
    total = None
    out = None
    for score, (keys, _, _, bias) in zip(scores, pieces):
        shift = new_max if bias is None else new_max - bias
        weights = jnp.exp2(score * scale - shift)
        part = jnp.sum(weights, axis=1, keepdims=True)
        update = jnp.dot(weights.astype(keys.dtype), keys, preferred_element_type=jnp.float32)
        total = part if total is None else total + part
        out = update if out is None else out + update
    if state is not None:
        factor = jnp.exp2(state[0] - new_max)
        total = total + state[1] * factor
        out = out + state[2] * factor
    return new_max, total, out


def own_kernel(block, heads, scale, rep_ref, query_hbm, qrope_ref, latent_hbm, rope_hbm, *refs):
    there_latent, there_rope, query_ref, max_ref, sum_ref, out_ref, latent_ref, rope_ref, sems = refs
    copies = [
        pltpu.make_async_copy(query_hbm, query_ref, sems.at[0]),
        pltpu.make_async_copy(latent_hbm, latent_ref, sems.at[1]),
        pltpu.make_async_copy(rope_hbm, rope_ref, sems.at[2]),
    ]
    for copy in copies:
        copy.start()
    for copy in copies:
        copy.wait()
    rows = query_ref.shape[0]
    half = latent_ref.shape[0]
    queries = rows // heads
    rep = rep_ref[0]

    for start in range(0, rows, block):
        rows_here = pl.ds(start, block)

        def causal(first, score):
            j = first + lax.broadcasted_iota(jnp.int32, score.shape, 1)
            q = (start + lax.broadcasted_iota(jnp.int32, score.shape, 0)) // heads
            return jnp.where(j <= 2 * half - queries + q, score, masked_score)

        pieces = [
            (latent_ref[...], rope_ref[...], functools.partial(causal, rep * half), None),
            (there_latent[...], there_rope[...], functools.partial(causal, (1 - rep) * half), None),
        ]
        state = attend_rows(rows_here, query_ref, qrope_ref, pieces, scale, None)
        max_ref[rows_here, :], sum_ref[rows_here, :], out_ref[rows_here, :] = state


def attention_cost(rows, keys, width):
    return pl.CostEstimate(
        flops=4 * rows * keys * width, bytes_accessed=2 * rows * width, transcendentals=rows * keys
    )


def attend_own(rep, query, query_rope, here, there, heads, scale):
    rows, width = query.shape
    out_shape = (
        jax.ShapeDtypeStruct(query.shape, query.dtype),
        jax.ShapeDtypeStruct((rows, 1), jnp.float32),
        jax.ShapeDtypeStruct((rows, 1), jnp.float32),
        jax.ShapeDtypeStruct((rows, width), jnp.float32),
    )
    query, *state = pl.pallas_call(
        functools.partial(own_kernel, math.gcd(rows, 256), heads, scale),
        out_shape=out_shape,
        in_specs=[in_smem, in_hbm, in_vmem, in_hbm, in_hbm, in_vmem, in_vmem],
        out_specs=[in_vmem] * 4,
        scratch_shapes=[
            pltpu.VMEM(here[0].shape, here[0].dtype),
            pltpu.VMEM(here[1].shape, here[1].dtype),
            pltpu.SemaphoreType.DMA((3,)),
        ],
        compiler_params=params(10),
        cost_estimate=attention_cost(rows, 2 * here[0].shape[0], width),
        name="attend_own",
    )(rep, kept_in_hbm(query), query_rope, *[kept_in_hbm(x) for x in here], *there)
    return query, state


def biased_pieces(counts, shard_ref, refs, rope_width):
    pieces = []
    first = 0
    for level, count in counts:
        keys, ropes = joined(refs[first : first + count], rope_width)
        first += count
        bias = jnp.where(shard_ref[0] >= 2**level, 0.0, masked_score)
        pieces.append((keys, ropes, None, bias))
    return pieces


def counted(refs_of):
    counts = tuple((level, len(refs)) for level, refs in sorted(refs_of.items()))
    return counts, [ref for _, refs in sorted(refs_of.items()) for ref in refs]


def middle_kernel(block, counts, scale, shard_ref, query_ref, qrope_ref, *refs):
    count = sum(count for _, count in counts)
    max_in, sum_in, out_in, max_ref, sum_ref, out_ref = refs[count:]
    pieces = biased_pieces(counts, shard_ref, refs[:count], qrope_ref.shape[1])
    for start in range(0, query_ref.shape[0], block):
        rows_here = pl.ds(start, block)
        state = (max_in[rows_here, :], sum_in[rows_here, :], out_in[rows_here, :])
        state = attend_rows(rows_here, query_ref, qrope_ref, pieces, scale, state)
        max_ref[rows_here, :], sum_ref[rows_here, :], out_ref[rows_here, :] = state


def attend_middle(shard, query, query_rope, refs_of, state, scale):
    rows, width = query.shape
    counts, refs = counted(refs_of)
    keys = sum(ref.shape[0] for ref in refs)
    return pl.pallas_call(
        functools.partial(middle_kernel, math.gcd(rows, 256), counts, scale),
        out_shape=tuple(jax.ShapeDtypeStruct(s.shape, s.dtype) for s in state),
        in_specs=[in_smem] + [in_vmem] * (2 + len(refs) + 3),
        out_specs=[in_vmem] * 3,
        compiler_params=params(12),
        cost_estimate=attention_cost(rows, keys, width),
    )(shard, query, query_rope, *refs, *state)


def last_kernel(
    block, counts, heads, scale, columns, column_ref, rep_ref, shard_ref, query_ref, qrope_ref, *refs
):
    count = sum(count for _, count in counts)
    max_in, sum_in, out_in, up_ref, proj_ref, result_ref, norm_ref, exp_ref = refs[count:]
    rows, width = query_ref.shape
    queries = rows // heads
    value = up_ref.shape[2]
    pieces = biased_pieces(counts, shard_ref, refs[:count], qrope_ref.shape[1])
    for start in range(0, rows, block):
        rows_here = pl.ds(start, block)
        state = (max_in[rows_here, :], sum_in[rows_here, :], out_in[rows_here, :])
        _, total, out = attend_rows(rows_here, query_ref, qrope_ref, pieces, scale, state)
        norm = out * (1.0 / total)
        for tile in range(width // lanes):
            norm_ref[tile, rows_here, :] = norm[:, tile * lanes : (tile + 1) * lanes]
    for head in range(heads):
        tiles = [
            norm_ref[tile, pl.ds(head, queries, stride=heads), :].astype(jnp.bfloat16)
            for tile in range(width // lanes)
        ]
        attended = jnp.concatenate(tiles, axis=1)
        expanded = jnp.dot(attended, up_ref[head], preferred_element_type=jnp.float32)
        exp_ref[:, pl.ds(head * value, value)] = expanded.astype(jnp.bfloat16)
    chunk = queries // (2 * columns)
    parts = []
    for core in (1 - rep_ref[0], rep_ref[0]):
        for by in range(1, columns + 1):
            owner = lax.rem(column_ref[0] + by, columns) * 2 + core
            parts.append(exp_ref[pl.ds(pl.multiple_of(owner * chunk, chunk), chunk), :])
    lhs = jnp.concatenate(parts, axis=0)
    width_out = proj_ref.shape[1]
    step = math.gcd(width_out, 512)
    for start in range(0, width_out, step):
        piece = jnp.dot(lhs, proj_ref[:, pl.ds(start, step)], preferred_element_type=jnp.float32)
        result_ref[:, pl.ds(start, step)] = piece.astype(result_ref.dtype)


def attend_last(
    columns, column, rep, shard, query, query_rope, refs_of, state, scale, value_up, out_proj
):
    counts, refs = counted(refs_of)
    rows, width = query.shape
    heads = value_up.shape[0]
    queries = rows // heads
    keys = sum(ref.shape[0] for ref in refs)
    width_out = out_proj.shape[1]
    return pl.pallas_call(
        functools.partial(
            last_kernel, math.gcd(rows, 256), counts, heads, scale, columns
        ),
        out_shape=jax.ShapeDtypeStruct((queries, width_out), jnp.bfloat16),
        in_specs=[in_smem] * 3 + [in_vmem] * (2 + len(refs) + 3 + 2),
        out_specs=in_vmem,
        scratch_shapes=[
            pltpu.VMEM((width // lanes, rows, lanes), jnp.float32),
            pltpu.VMEM((queries, out_proj.shape[0]), jnp.bfloat16),
        ],
        compiler_params=params(12),
        cost_estimate=attention_cost(rows, keys, width),
        name="attend_last",
    )(column, rep, shard, query, query_rope, *refs, *state, value_up, out_proj)


def shards(query_latent, query_rope, latent, key_rope, value_up, out_proj):
    queries, heads, width = query_latent.shape
    rope_width = key_rope.shape[0]
    levels = level_count(lax.axis_size("seq"))
    columns = lax.axis_size("head")
    column = lax.axis_index("head")[None]
    rep = lax.axis_index("rep")[None]
    shard = lax.axis_index("seq")[None]
    column, rep, shard = lax.optimization_barrier((column, rep, shard))
    scale = (width + rope_width) ** (-0.5) * log2e
    query = query_latent.reshape(queries * heads, width)
    qrope = query_rope.reshape(queries * heads, rope_width)

    chunks = chunk_count(latent.shape[0] // columns)
    direct = pack_part(column, columns, chunks, latent, key_rope)
    there = (rotated(latent, "rep", 1), rotated(key_rope, "rep", 1))
    query, state = attend_own(rep, query, qrope, (latent, key_rope), there, heads, scale)

    first, middle, last = {}, {}, {}
    for level in range(levels):
        by = 1 if level == 0 else 2 ** (level - 1)
        direct = [shifted(piece, "seq", by, 0 if level == 0 else by) for piece in direct]
        for chunk, piece in enumerate(direct):
            for index in range(columns):
                if index:
                    moved = rotated(piece, "head", index)
                else:
                    moved = piece
                both = [moved, rotated(moved, "rep", 1)]
                crossed = index > 0
                final = level == levels - 1 and crossed == (columns > 1)
                stage = last if final else middle if level or crossed else first
                stage.setdefault(level, []).extend(both)
    for refs_of in (first, middle):
        if refs_of:
            state = attend_middle(shard, query, qrope, refs_of, state, scale)
    partial = attend_last(
        columns, column, rep, shard, query, qrope, last, state, scale, value_up, out_proj
    )
    half = queries // 2
    arrived = rotated(partial[:half], "rep", 1)
    chunk = half // columns
    kept = partial[half:]
    sums = []
    for index in range(columns):
        rows = slice(index * chunk, (index + 1) * chunk)
        sums.append(kept[rows].astype(jnp.float32) + arrived[rows].astype(jnp.float32))
    result = sums[-1]
    for index in range(columns - 1):
        sent = sums[index].astype(jnp.bfloat16)
        result = result + rotated(sent, "head", index + 1).astype(jnp.float32)
    return result.astype(jnp.bfloat16)


def level_count(shards_along):
    return min(4, shards_along // 4 + 1)


def chunk_count(rows):
    return 2 if rows % (2 * lanes) == 0 else 1


def solution(mesh):
    placed = (
        P(("grp", "seq"), ("head", "rep"), None),
        P(("grp", "seq"), ("head", "rep")),
        P(("grp", "seq", "rep"), None),
        P(None, ("grp", "seq", "rep")),
        P(("head", "rep"), None, None),
        P(("head", "rep"), None),
    )

    return jax.shard_map(
        shards,
        mesh=mesh,
        in_specs=placed,
        out_specs=P(("grp", "seq", "head", "rep"), None),
        check_vma=False,
    )
```
